32 devices in a mesh: row: 4 (over x, core), col: 8 (over z, y).
Axes of the slice: x: 2, y: 2, z: 4, core: 2. Of those that a mesh axis runs over, the one named last changes fastest.
Arguments:
- pair: bfloat16 [768, 768, 512], P('row', 'col'), may hold values from -6 to 6
- w_bias: bfloat16 [512, 96], replicated, may hold values from -0.25 to 0.25
- queries: bfloat16 [768, 1536], P('row', 'col'), may hold values from -360 to 360
- keys: bfloat16 [768, 1536], P('col', 'row'), may hold values from -6 to 6
- values: bfloat16 [768, 1536], P('col', 'row'), may hold values from -6 to 6
- d_out: bfloat16 [768, 1536], P('row', 'col'), may hold values from -6 to 6
Outputs:
- d_pair: bfloat16 [768, 768, 512], P('row', 'col')
- d_wbias: float32 [512, 96], replicated
- d_queries: bfloat16 [768, 1536], P('row', 'col')
- d_keys: bfloat16 [768, 1536], P('col', 'row')
- d_values: bfloat16 [768, 1536], P('col', 'row')
The draws below stay inside these ranges and needn't reach their ends.
All inputs are finite; a program needn't handle non-finite values.
Results may differ from the reference program's by a relative error of at most 0.0095.
Values may be sent and summed in bfloat16 or wider, within the bound.
A program may use at most 128 MiB of HBM per device.

```python
import jax
import jax.numpy as jnp
from jax import lax

D = 1536
H = 96
P_SIZE = 512
N = 768
HD = 16


def draw_entries(key):
    base = jax.random.fold_in(key, 7101)
    query_key, key_key = jax.random.split(base, 2)
    query_draw = jnp.clip(jax.random.normal(query_key, (N, D), jnp.float32), -6.0, 6.0)
    key_draw = jnp.clip(jax.random.normal(key_key, (N, D), jnp.float32), -6.0, 6.0)
    return (query_draw, key_draw)


def draw_queries(key, part):
    return draw_entries(key)[0].astype(jnp.bfloat16)


def draw_keys(key, part):
    return draw_entries(key)[1].astype(jnp.bfloat16)


def block_scale(own_key, extent, cuts, least, largest):
    loudness, own = 1.0, jax.random.fold_in(own_key, 6)
    for axis_at, parts in cuts:
        heights = jnp.exp(jax.random.uniform(jax.random.fold_in(own, axis_at), (parts,), jnp.float32, least / len(cuts), largest / len(cuts)))
        loudness = loudness * jnp.repeat(heights, extent[axis_at] // parts).reshape([-1 if axis == axis_at else 1 for axis in range(len(extent))])
    return loudness


def scatter_about(key, dims, scale, limit, shards=(), held_as=jnp.bfloat16):
    gain = block_scale(key, dims, shards, -0.22, 0.18) if shards else 1.0
    drawn = jax.random.normal(key, dims, jnp.float32) * scale * gain
    return jnp.minimum(jnp.maximum(drawn, -limit), limit).astype(held_as)


def setup_inputs(seed: int = 0) -> dict:
    key_of = jax.random.split(jax.random.key(seed), 7)
    return {
        "pair": scatter_about(key_of[0], (N, N, P_SIZE), 1.0, 6.0, ((0, 4), (1, 8))),
        "w_bias": scatter_about(key_of[1], (P_SIZE, H), P_SIZE ** -0.5, 0.25),
        "queries": draw_queries(jax.random.fold_in(key_of[6], 71), 0),
        "keys": draw_keys(jax.random.fold_in(key_of[6], 71), 0),
        "values": scatter_about(key_of[4], (N, D), 1.0, 6.0, ((0, 8), (1, 4))),
        "d_out": scatter_about(key_of[5], (N, D), 1.0, 6.0, ((0, 4), (1, 8))),
    }


def reference(pair, w_bias, queries, keys, values, d_out):
    block_rows = N // 16
    scale = 1.0 / (HD ** 0.5)
    key_heads = keys.astype(jnp.float32).reshape(N, H, HD)
    value_heads = values.astype(jnp.float32).reshape(N, H, HD)

    def advance(totals, block_index):
        grad_keys, grad_values, grad_weight = totals
        offset = (block_index * block_rows).astype(jnp.int32)
        pair_block = lax.dynamic_slice_in_dim(pair, offset, block_rows, 0)
        query_heads = lax.dynamic_slice_in_dim(queries, offset, block_rows, 0).astype(jnp.float32).reshape(block_rows, H, HD)
        out_heads = lax.dynamic_slice_in_dim(d_out, offset, block_rows, 0).astype(jnp.float32).reshape(block_rows, H, HD)
        flat_pair = pair_block.reshape(block_rows * N, P_SIZE)
        pair_bias = jnp.dot(flat_pair, w_bias, preferred_element_type=jnp.float32).reshape(block_rows, N, H)
        scores = jnp.einsum('ihd,jhd->hij', query_heads, key_heads) * scale + pair_bias.transpose(2, 0, 1)
        weights = jax.nn.softmax(scores, axis=-1)
        grad_prob = jnp.einsum('ihd,jhd->hij', out_heads, value_heads)
        row_delta = jnp.sum(weights * grad_prob, axis=-1, keepdims=True)
        grad_score = (weights * (grad_prob - row_delta)).astype(jnp.bfloat16)
        weights_low = weights.astype(jnp.bfloat16)
        score_flat = grad_score.transpose(1, 2, 0).reshape(block_rows * N, H)
        pair_grad = jnp.dot(score_flat, w_bias.T, preferred_element_type=jnp.float32).astype(jnp.bfloat16).reshape(block_rows, N, P_SIZE)
        grad_weight = grad_weight + jnp.dot(flat_pair.T, score_flat, preferred_element_type=jnp.float32)
        score_wide = grad_score.astype(jnp.float32)
        query_grad = (jnp.einsum('hij,jhd->ihd', score_wide, key_heads) * scale).reshape(block_rows, D).astype(jnp.bfloat16)
        grad_keys = grad_keys + (jnp.einsum('hij,ihd->jhd', score_wide, query_heads) * scale).reshape(N, D)
        grad_values = grad_values + jnp.einsum('hij,ihd->jhd', weights_low.astype(jnp.float32), out_heads).reshape(N, D)
        return (grad_keys, grad_values, grad_weight), (pair_grad, query_grad)

    start_totals = (jnp.zeros((N, D), jnp.float32), jnp.zeros((N, D), jnp.float32), jnp.zeros((P_SIZE, H), jnp.float32))
    totals, pieces = lax.scan(advance, start_totals, jnp.arange(16, dtype=jnp.int32))
    d_pair = pieces[0].reshape(N, N, P_SIZE)
    d_queries = pieces[1].reshape(N, D)
    return d_pair, totals[2], d_queries, totals[0].astype(jnp.bfloat16), totals[1].astype(jnp.bfloat16)
```

```python
import functools

import jax
import jax.numpy as jnp
from jax import lax
from jax.experimental import pallas as pl
from jax.experimental.pallas import tpu as pltpu
from jax.sharding import PartitionSpec as P

H = 96
HD = 16
SCALE = 1.0 / HD**0.5
MESH = pl.DeviceIdType.MESH
VMEM = pltpu.VMEM
DMA = pltpu.SemaphoreType.DMA


def remote(src, dst, send, recv, row, col):
    return pltpu.make_async_remote_copy(
        src_ref=src, dst_ref=dst, send_sem=send, recv_sem=recv,
        device_id=(row, col), device_id_type=MESH,
    )


def greet(nrow, ncol, row, col):
    barrier = pltpu.get_barrier_semaphore()
    for k in range(1, ncol):
        pl.semaphore_signal(
            barrier, inc=1, device_id=(row, lax.rem(col + k, ncol)), device_id_type=MESH
        )
    for k in range(1, nrow):
        pl.semaphore_signal(
            barrier, inc=1, device_id=(lax.rem(row + k, nrow), col), device_id_type=MESH
        )
    pl.semaphore_wait(barrier, ncol + nrow - 2)


def gather_kernel(nrow, ncol, qd, kv, qd_all, kv_all, qs, qr, fs, fr, ks, kr):
    row, col = lax.axis_index("row"), lax.axis_index("col")
    inner = 2 if ncol % 2 == 0 else 1
    outer = ncol // inner
    a, b = col // inner, lax.rem(col, inner)
    greet(nrow, ncol, row, col)
    sends = []
    for k in range(1, outer):
        to = lax.rem(a + k, outer) * inner + b
        sends.append(remote(qd, qd_all.at[col], qs.at[k], qr.at[k], row, to))
    if inner == 2:
        sends.append(remote(qd, qd_all.at[col], fs.at[0], fr.at[0], row, a * inner + 1 - b))
    for k in range(1, nrow):
        sends.append(remote(kv, kv_all.at[row], ks.at[k], kr.at[k], lax.rem(row + k, nrow), col))
    for copy in sends:
        copy.start()
    qd_all[col] = qd[...]
    kv_all[row] = kv[...]
    for k in range(1, outer):
        src = lax.rem(a + outer - k, outer) * inner + b
        remote(qd, qd_all.at[src], qs.at[k], qr.at[k], row, col).wait_recv()
        if inner == 2:
            copy = remote(
                qd_all.at[src], qd_all.at[src], fs.at[k], fr.at[k], row, a * inner + 1 - b
            )
            copy.start()
            sends.append(copy)
    if inner == 2:
        for k in range(outer):
            src = lax.rem(a + outer - k, outer) * inner + 1 - b
            remote(qd, qd_all.at[src], fs.at[k], fr.at[k], row, col).wait_recv()
    for k in range(1, nrow):
        src = lax.rem(row + nrow - k, nrow)
        remote(kv, kv_all.at[src], ks.at[k], kr.at[k], row, col).wait_recv()
    for copy in sends:
        copy.wait_send()


def gather(nrow, ncol, qd, kv):
    return pl.pallas_call(
        functools.partial(gather_kernel, nrow, ncol),
        out_shape=(
            jax.ShapeDtypeStruct((ncol,) + qd.shape, qd.dtype),
            jax.ShapeDtypeStruct((nrow,) + kv.shape, kv.dtype),
        ),
        in_specs=[pl.BlockSpec(memory_space=VMEM)] * 2,
        out_specs=[pl.BlockSpec(memory_space=VMEM)] * 2,
        scratch_shapes=[DMA((ncol,))] * 4 + [DMA((nrow,))] * 2,
        compiler_params=pltpu.CompilerParams(collective_id=0, has_side_effects=True),
    )(qd, kv)


def stats_kernel(ncol, st, out, got, back, s1, r1, s2, r2):
    row, col = lax.axis_index("row"), lax.axis_index("col")
    barrier = pltpu.get_barrier_semaphore()
    for k in range(1, ncol):
        pl.semaphore_signal(
            barrier, inc=1, device_id=(row, lax.rem(col + k, ncol)), device_id_type=MESH
        )
    pl.semaphore_wait(barrier, ncol - 1)
    sends = []
    for k in range(1, ncol):
        to = lax.rem(col + k, ncol)
        copy = remote(st.at[to], got.at[k], s1.at[k], r1.at[k], row, to)
        copy.start()
        sends.append(copy)
    got[0] = st[col]
    for k in range(1, ncol):
        remote(st.at[k], got.at[k], s1.at[k], r1.at[k], row, col).wait_recv()
    top = got[0, 0]
    for k in range(1, ncol):
        top = jnp.maximum(top, got[k, 0])
    total = jnp.zeros_like(top)
    upper = jnp.zeros_like(top)
    scales = []
    for k in range(ncol):
        scale = jnp.exp(got[k, 0] - top)
        scales.append(scale)
        total += got[k, 1] * scale
        upper += got[k, 2] * scale
    delta = upper / total
    for k in range(ncol):
        back[k, 0] = scales[k] / total
        back[k, 1] = delta
    for k in range(1, ncol):
        to = lax.rem(col + ncol - k, ncol)
        copy = remote(back.at[k], out.at[col], s2.at[k], r2.at[k], row, to)
        copy.start()
        sends.append(copy)
    out[col] = back[0]
    for k in range(1, ncol):
        src = lax.rem(col + k, ncol)
        remote(back.at[k], out.at[src], s2.at[k], r2.at[k], row, col).wait_recv()
    for copy in sends:
        copy.wait_send()


def stats(ncol, st):
    part = st.shape[2:]
    return pl.pallas_call(
        functools.partial(stats_kernel, ncol),
        out_shape=jax.ShapeDtypeStruct((ncol, 2) + part, jnp.float32),
        in_specs=[pl.BlockSpec(memory_space=VMEM)],
        out_specs=pl.BlockSpec(memory_space=VMEM),
        scratch_shapes=[
            VMEM((ncol, 3) + part, jnp.float32),
            VMEM((ncol, 2) + part, jnp.float32),
        ]
        + [DMA((ncol,))] * 4,
        compiler_params=pltpu.CompilerParams(collective_id=1, has_side_effects=True),
    )(st)


def reduce_kernel(
    nrow, ncol, wb, dq, dkv, wb_out, q_out, kv_out,
    w1, w1sum, w2, w2sum, qgot, kgot, ws1, wr1, ws2, wr2, ws3, wr3, ws4, wr4, qs, qr, ks, kr,
):
    row, col = lax.axis_index("row"), lax.axis_index("col")
    greet(nrow, ncol, row, col)
    sends = []

    def go(copy):
        copy.start()
        sends.append(copy)

    for k in range(1, nrow):
        to = lax.rem(row + k, nrow)
        go(remote(wb.at[to], w1.at[k], ws1.at[k], wr1.at[k], to, col))
    for k in range(1, ncol):
        to = lax.rem(col + k, ncol)
        go(remote(dq.at[to], qgot.at[k], qs.at[k], qr.at[k], row, to))
    for k in range(1, nrow):
        to = lax.rem(row + k, nrow)
        go(remote(dkv.at[to], kgot.at[k], ks.at[k], kr.at[k], to, col))
    total = wb[row]
    for k in range(1, nrow):
        remote(wb.at[0], w1.at[k], ws1.at[k], wr1.at[k], row, col).wait_recv()
        total += w1[k]
    w1sum[...] = total
    for k in range(1, ncol):
        to = lax.rem(col + k, ncol)
        go(remote(w1sum.at[to], w2.at[k], ws2.at[k], wr2.at[k], row, to))
    part = w1sum[col]
    for k in range(1, ncol):
        remote(w1sum.at[0], w2.at[k], ws2.at[k], wr2.at[k], row, col).wait_recv()
        part += w2[k]
    w2sum[...] = part
    for k in range(1, ncol):
        to = lax.rem(col + k, ncol)
        go(remote(w2sum, wb_out.at[row, col], ws3.at[k], wr3.at[k], row, to))
    wb_out[row, col] = part
    for k in range(1, ncol):
        src = lax.rem(col + ncol - k, ncol)
        remote(w2sum, wb_out.at[row, src], ws3.at[k], wr3.at[k], row, col).wait_recv()
    for k in range(1, nrow):
        to = lax.rem(row + k, nrow)
        go(remote(wb_out.at[row], wb_out.at[row], ws4.at[k], wr4.at[k], to, col))
    grad = dkv[row].astype(jnp.float32)
    for k in range(1, nrow):
        remote(dkv.at[0], kgot.at[k], ks.at[k], kr.at[k], row, col).wait_recv()
        grad += kgot[k].astype(jnp.float32)
    kv_out[...] = grad.astype(kv_out.dtype)
    grad = dq[col].astype(jnp.float32)
    for k in range(1, ncol):
        remote(dq.at[0], qgot.at[k], qs.at[k], qr.at[k], row, col).wait_recv()
        grad += qgot[k].astype(jnp.float32)
    q_out[...] = grad.astype(q_out.dtype)
    for k in range(1, nrow):
        src = lax.rem(row + nrow - k, nrow)
        remote(wb_out.at[src], wb_out.at[src], ws4.at[k], wr4.at[k], row, col).wait_recv()
    for copy in sends:
        copy.wait_send()


def reduce_all(nrow, ncol, wb, dq, dkv):
    chunk = wb.shape[2:]
    return pl.pallas_call(
        functools.partial(reduce_kernel, nrow, ncol),
        out_shape=(
            jax.ShapeDtypeStruct(wb.shape, jnp.float32),
            jax.ShapeDtypeStruct(dq.shape[1:], jnp.bfloat16),
            jax.ShapeDtypeStruct(dkv.shape[1:], jnp.bfloat16),
        ),
        in_specs=[pl.BlockSpec(memory_space=VMEM)] * 3,
        out_specs=[pl.BlockSpec(memory_space=VMEM)] * 3,
        scratch_shapes=[
            VMEM(wb.shape, jnp.float32),
            VMEM((ncol,) + chunk, jnp.float32),
            VMEM((ncol,) + chunk, jnp.float32),
            VMEM(chunk, jnp.float32),
            VMEM(dq.shape, dq.dtype),
            VMEM(dkv.shape, dkv.dtype),
            DMA((nrow,)), DMA((nrow,)), DMA((ncol,)), DMA((ncol,)),
            DMA((ncol,)), DMA((ncol,)), DMA((nrow,)), DMA((nrow,)),
            DMA((ncol,)), DMA((ncol,)), DMA((nrow,)), DMA((nrow,)),
        ],
        compiler_params=pltpu.CompilerParams(collective_id=2, has_side_effects=True),
    )(wb, dq, dkv)


def on_device(nrow, ncol, pair, w_bias, queries, keys, values, d_out):
    R, C, width = pair.shape
    dcol, drow = queries.shape[1], keys.shape[1]
    qd_all, kv_all = gather(
        nrow, ncol,
        jnp.concatenate([queries, d_out], axis=1),
        jnp.concatenate([keys, values], axis=1),
    )
    query_heads = qd_all[:, :, :dcol].transpose(1, 0, 2).reshape(R, H, HD)
    out_heads = qd_all[:, :, dcol:].transpose(1, 0, 2).reshape(R, H, HD)
    key_heads = kv_all[:, :, :drow].transpose(1, 0, 2).reshape(C, H, HD)
    value_heads = kv_all[:, :, drow:].transpose(1, 0, 2).reshape(C, H, HD)
    flat_pair = pair.reshape(R * C, width)
    pair_bias = jnp.dot(flat_pair, w_bias, preferred_element_type=jnp.float32).reshape(R, C, H)
    scores = jnp.einsum(
        "ihd,jhd->hij", query_heads, key_heads, preferred_element_type=jnp.float32
    ) * SCALE + pair_bias.transpose(2, 0, 1)
    grad_prob = jnp.einsum(
        "ihd,jhd->hij", out_heads, value_heads, preferred_element_type=jnp.float32
    )
    local_max = jnp.max(scores, axis=-1)
    exp_scores = jnp.exp(scores - local_max[..., None])
    st = jnp.stack(
        [local_max, jnp.sum(exp_scores, axis=-1), jnp.sum(exp_scores * grad_prob, axis=-1)]
    )
    st = st.reshape(3, ncol, H // ncol, R).transpose(1, 0, 2, 3)
    back = stats(ncol, st).transpose(1, 0, 2, 3).reshape(2, H, R)
    weights = exp_scores * back[0][..., None]
    grad_score = (weights * (grad_prob - back[1][..., None])).astype(jnp.bfloat16)
    weights_low = weights.astype(jnp.bfloat16)
    score_flat = grad_score.transpose(1, 2, 0).reshape(R * C, H)
    d_pair = (
        jnp.dot(score_flat, w_bias.T, preferred_element_type=jnp.float32)
        .astype(jnp.bfloat16)
        .reshape(R, C, width)
    )
    weight_term = jnp.dot(score_flat.T, flat_pair, preferred_element_type=jnp.float32)
    query_term = jnp.einsum(
        "hij,jhd->ihd", grad_score, key_heads, preferred_element_type=jnp.float32
    ) * SCALE
    key_term = jnp.einsum(
        "hij,ihd->jhd", grad_score, query_heads, preferred_element_type=jnp.float32
    ) * SCALE
    value_term = jnp.einsum(
        "hij,ihd->jhd", weights_low, out_heads, preferred_element_type=jnp.float32
    )
    dq = query_term.astype(jnp.bfloat16).reshape(R, ncol, dcol).transpose(1, 0, 2)
    dk = key_term.astype(jnp.bfloat16).reshape(C, nrow, drow).transpose(1, 0, 2)
    dv = value_term.astype(jnp.bfloat16).reshape(C, nrow, drow).transpose(1, 0, 2)
    wb = weight_term.reshape(ncol, H // ncol, nrow, width // nrow).transpose(2, 0, 1, 3)
    wb, q_grad, kv_grad = reduce_all(nrow, ncol, wb, dq, jnp.concatenate([dk, dv], axis=2))
    d_wbias = wb.transpose(0, 3, 1, 2).reshape(width, H)
    return d_pair, d_wbias, q_grad, kv_grad[:, :drow], kv_grad[:, drow:]


def solution(mesh):
    return jax.shard_map(
        functools.partial(on_device, mesh.shape["row"], mesh.shape["col"]),
        mesh=mesh,
        in_specs=(
            P("row", "col", None),
            P(),
            P("row", "col"),
            P("col", "row"),
            P("col", "row"),
            P("row", "col"),
        ),
        out_specs=(P("row", "col", None), P(), P("row", "col"), P("col", "row"), P("col", "row")),
        check_vma=False,
    )
```

```python
import functools

import jax
import jax.numpy as jnp
from jax import lax
from jax.experimental import pallas as pl
from jax.experimental.pallas import tpu as pltpu
from jax.sharding import PartitionSpec as P

H = 96
HD = 16
SCALE = 1.0 / HD**0.5
MESH = pl.DeviceIdType.MESH
VMEM = pltpu.VMEM
DMA = pltpu.SemaphoreType.DMA


def remote(src, dst, send, recv, row, col):
    return pltpu.make_async_remote_copy(
        src_ref=src, dst_ref=dst, send_sem=send, recv_sem=recv,
        device_id=(row, col), device_id_type=MESH,
    )


def greet(nrow, ncol, row, col):
    barrier = pltpu.get_barrier_semaphore()
    for k in range(1, ncol):
        pl.semaphore_signal(
            barrier, inc=1, device_id=(row, lax.rem(col + k, ncol)), device_id_type=MESH
        )
    for k in range(1, nrow):
        pl.semaphore_signal(
            barrier, inc=1, device_id=(lax.rem(row + k, nrow), col), device_id_type=MESH
        )
    pl.semaphore_wait(barrier, ncol + nrow - 2)


def gather_kernel(nrow, ncol, qd, kv, qd_all, kv_all, qs, qr, fs, fr, ks, kr):
    row, col = lax.axis_index("row"), lax.axis_index("col")
    inner = 2 if ncol % 2 == 0 else 1
    outer = ncol // inner
    a, b = col // inner, lax.rem(col, inner)
    greet(nrow, ncol, row, col)
    sends = []
    for k in range(1, outer):
        to = lax.rem(a + k, outer) * inner + b
        sends.append(remote(qd, qd_all.at[col], qs.at[k], qr.at[k], row, to))
    if inner == 2:
        sends.append(remote(qd, qd_all.at[col], fs.at[0], fr.at[0], row, a * inner + 1 - b))
    for k in range(1, nrow):
        sends.append(remote(kv, kv_all.at[row], ks.at[k], kr.at[k], lax.rem(row + k, nrow), col))
    for copy in sends:
        copy.start()
    qd_all[col] = qd[...]
    kv_all[row] = kv[...]
    for k in range(1, outer):
        src = lax.rem(a + outer - k, outer) * inner + b
        remote(qd, qd_all.at[src], qs.at[k], qr.at[k], row, col).wait_recv()
        if inner == 2:
            copy = remote(
                qd_all.at[src], qd_all.at[src], fs.at[k], fr.at[k], row, a * inner + 1 - b
            )
            copy.start()
            sends.append(copy)
    if inner == 2:
        for k in range(outer):
            src = lax.rem(a + outer - k, outer) * inner + 1 - b
            remote(qd, qd_all.at[src], fs.at[k], fr.at[k], row, col).wait_recv()
    for k in range(1, nrow):
        src = lax.rem(row + nrow - k, nrow)
        remote(kv, kv_all.at[src], ks.at[k], kr.at[k], row, col).wait_recv()
    for copy in sends:
        copy.wait_send()


def gather(nrow, ncol, qd, kv):
    return pl.pallas_call(
        functools.partial(gather_kernel, nrow, ncol),
        out_shape=(
            jax.ShapeDtypeStruct((ncol,) + qd.shape, qd.dtype),
            jax.ShapeDtypeStruct((nrow,) + kv.shape, kv.dtype),
        ),
        in_specs=[pl.BlockSpec(memory_space=VMEM)] * 2,
        out_specs=[pl.BlockSpec(memory_space=VMEM)] * 2,
        scratch_shapes=[DMA((ncol,))] * 4 + [DMA((nrow,))] * 2,
        compiler_params=pltpu.CompilerParams(collective_id=0, has_side_effects=True),
    )(qd, kv)


def stats_kernel(ncol, st, out, got, back, s1, r1, s2, r2):
    row, col = lax.axis_index("row"), lax.axis_index("col")
    barrier = pltpu.get_barrier_semaphore()
    for k in range(1, ncol):
        pl.semaphore_signal(
            barrier, inc=1, device_id=(row, lax.rem(col + k, ncol)), device_id_type=MESH
        )
    pl.semaphore_wait(barrier, ncol - 1)
    sends = []
    for k in range(1, ncol):
        to = lax.rem(col + k, ncol)
        copy = remote(st.at[to], got.at[k], s1.at[k], r1.at[k], row, to)
        copy.start()
        sends.append(copy)
    got[0] = st[col]
    for k in range(1, ncol):
        remote(st.at[k], got.at[k], s1.at[k], r1.at[k], row, col).wait_recv()
    top = got[0, 0]
    for k in range(1, ncol):
        top = jnp.maximum(top, got[k, 0])
    total = jnp.zeros_like(top)
    upper = jnp.zeros_like(top)
    scales = []
    for k in range(ncol):
        scale = jnp.exp(got[k, 0] - top)
        scales.append(scale)
        total += got[k, 1] * scale
        upper += got[k, 2] * scale
    delta = upper / total
    for k in range(ncol):
        back[k, 0] = scales[k] / total
        back[k, 1] = delta
    for k in range(1, ncol):
        to = lax.rem(col + ncol - k, ncol)
        copy = remote(back.at[k], out.at[col], s2.at[k], r2.at[k], row, to)
        copy.start()
        sends.append(copy)
    out[col] = back[0]
    for k in range(1, ncol):
        src = lax.rem(col + k, ncol)
        remote(back.at[k], out.at[src], s2.at[k], r2.at[k], row, col).wait_recv()
    for copy in sends:
        copy.wait_send()


def stats(ncol, st):
    part = st.shape[2:]
    return pl.pallas_call(
        functools.partial(stats_kernel, ncol),
        out_shape=jax.ShapeDtypeStruct((ncol, 2) + part, jnp.float32),
        in_specs=[pl.BlockSpec(memory_space=VMEM)],
        out_specs=pl.BlockSpec(memory_space=VMEM),
        scratch_shapes=[
            VMEM((ncol, 3) + part, jnp.float32),
            VMEM((ncol, 2) + part, jnp.float32),
        ]
        + [DMA((ncol,))] * 4,
        compiler_params=pltpu.CompilerParams(collective_id=1, has_side_effects=True),
    )(st)


def reduce_kernel(
    nrow, ncol, wb, dq, dkv, wb_out, q_out, kv_out,
    w1, w1sum, w2, w2sum, qgot, kgot, ws1, wr1, ws2, wr2, ws3, wr3, ws4, wr4, qs, qr, ks, kr,
):
    row, col = lax.axis_index("row"), lax.axis_index("col")
    greet(nrow, ncol, row, col)
    sends = []

    def go(copy):
        copy.start()
        sends.append(copy)

    for k in range(1, nrow):
        to = lax.rem(row + k, nrow)
        go(remote(wb.at[to], w1.at[k], ws1.at[k], wr1.at[k], to, col))
    for k in range(1, ncol):
        to = lax.rem(col + k, ncol)
        go(remote(dq.at[to], qgot.at[k], qs.at[k], qr.at[k], row, to))
    for k in range(1, nrow):
        to = lax.rem(row + k, nrow)
        go(remote(dkv.at[to], kgot.at[k], ks.at[k], kr.at[k], to, col))
    total = wb[row]
    for k in range(1, nrow):
        remote(wb.at[0], w1.at[k], ws1.at[k], wr1.at[k], row, col).wait_recv()
        total += w1[k]
    w1sum[...] = total
    for k in range(1, ncol):
        to = lax.rem(col + k, ncol)
        go(remote(w1sum.at[to], w2.at[k], ws2.at[k], wr2.at[k], row, to))
    part = w1sum[col]
    for k in range(1, ncol):
        remote(w1sum.at[0], w2.at[k], ws2.at[k], wr2.at[k], row, col).wait_recv()
        part += w2[k]
    w2sum[...] = part
    for k in range(1, ncol):
        to = lax.rem(col + k, ncol)
        go(remote(w2sum, wb_out.at[row, col], ws3.at[k], wr3.at[k], row, to))
    wb_out[row, col] = part
    for k in range(1, ncol):
        src = lax.rem(col + ncol - k, ncol)
        remote(w2sum, wb_out.at[row, src], ws3.at[k], wr3.at[k], row, col).wait_recv()
    for k in range(1, nrow):
        to = lax.rem(row + k, nrow)
        go(remote(wb_out.at[row], wb_out.at[row], ws4.at[k], wr4.at[k], to, col))
    grad = dkv[row].astype(jnp.float32)
    for k in range(1, nrow):
        remote(dkv.at[0], kgot.at[k], ks.at[k], kr.at[k], row, col).wait_recv()
        grad += kgot[k].astype(jnp.float32)
    kv_out[...] = grad.astype(kv_out.dtype)
    grad = dq[col].astype(jnp.float32)
    for k in range(1, ncol):
        remote(dq.at[0], qgot.at[k], qs.at[k], qr.at[k], row, col).wait_recv()
        grad += qgot[k].astype(jnp.float32)
    q_out[...] = grad.astype(q_out.dtype)
    for k in range(1, nrow):
        src = lax.rem(row + nrow - k, nrow)
        remote(wb_out.at[src], wb_out.at[src], ws4.at[k], wr4.at[k], row, col).wait_recv()
    for copy in sends:
        copy.wait_send()


def reduce_all(nrow, ncol, wb, dq, dkv):
    chunk = wb.shape[2:]
    return pl.pallas_call(
        functools.partial(reduce_kernel, nrow, ncol),
        out_shape=(
            jax.ShapeDtypeStruct(wb.shape, jnp.float32),
            jax.ShapeDtypeStruct(dq.shape[1:], jnp.bfloat16),
            jax.ShapeDtypeStruct(dkv.shape[1:], jnp.bfloat16),
        ),
        in_specs=[pl.BlockSpec(memory_space=VMEM)] * 3,
        out_specs=[pl.BlockSpec(memory_space=VMEM)] * 3,
        scratch_shapes=[
            VMEM(wb.shape, jnp.float32),
            VMEM((ncol,) + chunk, jnp.float32),
            VMEM((ncol,) + chunk, jnp.float32),
            VMEM(chunk, jnp.float32),
            VMEM(dq.shape, dq.dtype),
            VMEM(dkv.shape, dkv.dtype),
            DMA((nrow,)), DMA((nrow,)), DMA((ncol,)), DMA((ncol,)),
            DMA((ncol,)), DMA((ncol,)), DMA((nrow,)), DMA((nrow,)),
            DMA((ncol,)), DMA((ncol,)), DMA((nrow,)), DMA((nrow,)),
        ],
        compiler_params=pltpu.CompilerParams(collective_id=2, has_side_effects=True),
    )(wb, dq, dkv)


def bias_kernel(wt, pair, out):
    rows = pair.shape[0]
    out[...] = jnp.swapaxes(
        jnp.stack(
            [
                lax.dot_general(
                    wt[...], pair[k], (((1,), (1,)), ((), ())),
                    preferred_element_type=jnp.float32,
                )
                for k in range(rows)
            ]
        ),
        0, 1,
    )


def bias(pair, wt, block=8):
    R, C, width = pair.shape
    heads = wt.shape[0]
    return pl.pallas_call(
        bias_kernel,
        grid=(R // block,),
        out_shape=jax.ShapeDtypeStruct((heads, R, C), jnp.float32),
        in_specs=[
            pl.BlockSpec((heads, width), lambda i: (0, 0)),
            pl.BlockSpec((block, C, width), lambda i: (i, 0, 0)),
        ],
        out_specs=pl.BlockSpec((heads, block, C), lambda i: (0, i, 0)),
    )(wt, pair)


def pair_grad_kernel(wt, pair, ds, d_pair, wb):
    rows = pair.shape[0]
    by_row = jnp.swapaxes(ds[...].astype(jnp.float32), 0, 1).astype(jnp.bfloat16)

    @pl.when(pl.program_id(0) == 0)
    def _():
        wb[...] = jnp.zeros_like(wb)

    total = wb[...]
    for k in range(rows):
        one = by_row[k]
        d_pair[k] = lax.dot_general(
            one, wt[...], (((0,), (0,)), ((), ())), preferred_element_type=jnp.float32
        ).astype(jnp.bfloat16)
        total += jnp.dot(one, pair[k], preferred_element_type=jnp.float32)
    wb[...] = total


def pair_grad(pair, wt, ds, block=16):
    R, C, width = pair.shape
    heads = wt.shape[0]
    return pl.pallas_call(
        pair_grad_kernel,
        grid=(R // block,),
        out_shape=(
            jax.ShapeDtypeStruct(pair.shape, jnp.bfloat16),
            jax.ShapeDtypeStruct((heads, width), jnp.float32),
        ),
        in_specs=[
            pl.BlockSpec((heads, width), lambda i: (0, 0)),
            pl.BlockSpec((block, C, width), lambda i: (i, 0, 0)),
            pl.BlockSpec((heads, block, C), lambda i: (0, i, 0)),
        ],
        out_specs=(
            pl.BlockSpec((block, C, width), lambda i: (i, 0, 0)),
            pl.BlockSpec((heads, width), lambda i: (0, 0)),
        ),
    )(wt, pair, ds)


def on_device(nrow, ncol, pair, w_bias, queries, keys, values, d_out):
    R, C, width = pair.shape
    dcol, drow = queries.shape[1], keys.shape[1]
    qd_all, kv_all = gather(
        nrow, ncol,
        jnp.concatenate([queries, d_out], axis=1),
        jnp.concatenate([keys, values], axis=1),
    )
    query_heads = qd_all[:, :, :dcol].transpose(1, 0, 2).reshape(R, H, HD)
    out_heads = qd_all[:, :, dcol:].transpose(1, 0, 2).reshape(R, H, HD)
    key_heads = kv_all[:, :, :drow].transpose(1, 0, 2).reshape(C, H, HD)
    value_heads = kv_all[:, :, drow:].transpose(1, 0, 2).reshape(C, H, HD)
    wt = w_bias.T
    pair_bias = bias(pair, wt)
    scores = jnp.einsum(
        "ihd,jhd->hij", query_heads, key_heads, preferred_element_type=jnp.float32
    ) * SCALE + pair_bias
    grad_prob = jnp.einsum(
        "ihd,jhd->hij", out_heads, value_heads, preferred_element_type=jnp.float32
    )
    local_max = jnp.max(scores, axis=-1)
    exp_scores = jnp.exp(scores - local_max[..., None])
    st = jnp.stack(
        [local_max, jnp.sum(exp_scores, axis=-1), jnp.sum(exp_scores * grad_prob, axis=-1)]
    )
    count = H // ncol * R
    lanes = 128 if count % 128 == 0 else R
    st = st.reshape(3, ncol, count // lanes, lanes).transpose(1, 0, 2, 3)
    back = stats(ncol, st).transpose(1, 0, 2, 3).reshape(2, H, R)
    weights = exp_scores * back[0][..., None]
    grad_score = (weights * (grad_prob - back[1][..., None])).astype(jnp.bfloat16)
    weights_low = weights.astype(jnp.bfloat16)
    d_pair, weight_term = pair_grad(pair, wt, grad_score)
    query_term = jnp.einsum(
        "hij,jhd->ihd", grad_score, key_heads, preferred_element_type=jnp.float32
    ) * SCALE
    key_term = jnp.einsum(
        "hij,ihd->jhd", grad_score, query_heads, preferred_element_type=jnp.float32
    ) * SCALE
    value_term = jnp.einsum(
        "hij,ihd->jhd", weights_low, out_heads, preferred_element_type=jnp.float32
    )
    dq = query_term.astype(jnp.bfloat16).reshape(R, ncol, dcol).transpose(1, 0, 2)
    if R * dcol % 2048 == 0:
        dq = dq.reshape(ncol, R * dcol // 128, 128)
    dk = key_term.astype(jnp.bfloat16).reshape(C, nrow, drow).transpose(1, 0, 2)
    dv = value_term.astype(jnp.bfloat16).reshape(C, nrow, drow).transpose(1, 0, 2)
    wb = weight_term.reshape(ncol, H // ncol, nrow, width // nrow).transpose(2, 0, 1, 3)
    wb, q_grad, kv_grad = reduce_all(nrow, ncol, wb, dq, jnp.concatenate([dk, dv], axis=2))
    d_wbias = wb.transpose(0, 3, 1, 2).reshape(width, H)
    return d_pair, d_wbias, q_grad.reshape(R, dcol), kv_grad[:, :drow], kv_grad[:, drow:]


def solution(mesh):
    return jax.shard_map(
        functools.partial(on_device, mesh.shape["row"], mesh.shape["col"]),
        mesh=mesh,
        in_specs=(
            P("row", "col", None),
            P(),
            P("row", "col"),
            P("col", "row"),
            P("col", "row"),
            P("row", "col"),
        ),
        out_specs=(P("row", "col", None), P(), P("row", "col"), P("col", "row"), P("col", "row")),
        check_vma=False,
    )
```

```python
import functools

import jax
import jax.numpy as jnp
from jax import lax
from jax.experimental import pallas as pl
from jax.experimental.pallas import tpu as pltpu
from jax.sharding import PartitionSpec as P

H = 96
HD = 16
SCALE = 1.0 / HD**0.5
MESH = pl.DeviceIdType.MESH
VMEM = pltpu.VMEM
DMA = pltpu.SemaphoreType.DMA


def remote(src, dst, send, recv, row, col):
    return pltpu.make_async_remote_copy(
        src_ref=src, dst_ref=dst, send_sem=send, recv_sem=recv,
        device_id=(row, col), device_id_type=MESH,
    )


def greet(nrow, ncol, row, col):
    barrier = pltpu.get_barrier_semaphore()
    for k in range(1, ncol):
        pl.semaphore_signal(
            barrier, inc=1, device_id=(row, lax.rem(col + k, ncol)), device_id_type=MESH
        )
    for k in range(1, nrow):
        pl.semaphore_signal(
            barrier, inc=1, device_id=(lax.rem(row + k, nrow), col), device_id_type=MESH
        )
    pl.semaphore_wait(barrier, ncol + nrow - 2)


def gather_kernel(
    nrow, ncol, wt, pair, qd, kv, out, qd_all, kv_all, qs, qr, fs, fr, ks, kr, own
):
    row, col = lax.axis_index("row"), lax.axis_index("col")
    inner = 2 if ncol % 2 == 0 else 1
    outer = ncol // inner
    a, b = col // inner, lax.rem(col, inner)
    flip = a * inner + inner - 1 - b
    step, last = pl.program_id(0), pl.num_programs(0) - 1
    steps = out.shape[1]

    def sends():
        copies = []
        for k in range(1, outer):
            to = lax.rem(a + k, outer) * inner + b
            copies.append(remote(qd, qd_all.at[col], qs.at[k], qr.at[k], row, to))
        if inner == 2:
            copies.append(remote(qd, qd_all.at[col], fs.at[0], fr.at[0], row, flip))
        for k in range(1, nrow):
            to = lax.rem(row + k, nrow)
            copies.append(remote(kv, kv_all.at[row], ks.at[k], kr.at[k], to, col))
        copies.append(pltpu.make_async_copy(qd, qd_all.at[col], own.at[0]))
        copies.append(pltpu.make_async_copy(kv, kv_all.at[row], own.at[1]))
        return copies

    def relay(k):
        src = lax.rem(a + outer - k, outer) * inner + b
        return remote(qd_all.at[src], qd_all.at[src], fs.at[k], fr.at[k], row, flip)

    @pl.when(step == 0)
    def _():
        greet(nrow, ncol, row, col)
        for copy in sends():
            copy.start()

    out[...] = jnp.swapaxes(
        jnp.stack(
            [
                lax.dot_general(
                    wt[...], pair[k], (((1,), (1,)), ((), ())),
                    preferred_element_type=jnp.float32,
                )
                for k in range(steps)
            ]
        ),
        0, 1,
    )

    for k in range(1, outer):

        @pl.when(step == jnp.minimum(last, (last + 1) // 2 + 2 * (k - 1)))
        def _():
            src = lax.rem(a + outer - k, outer) * inner + b
            remote(qd, qd_all.at[src], qs.at[k], qr.at[k], row, col).wait_recv()
            if inner == 2:
                relay(k).start()

    @pl.when(step == last)
    def _():
        if inner == 2:
            for k in range(outer):
                src = lax.rem(a + outer - k, outer) * inner + 1 - b
                remote(qd, qd_all.at[src], fs.at[k], fr.at[k], row, col).wait_recv()
        for k in range(1, nrow):
            src = lax.rem(row + nrow - k, nrow)
            remote(kv, kv_all.at[src], ks.at[k], kr.at[k], row, col).wait_recv()
        copies = sends()
        for copy in copies[:-2]:
            copy.wait_send()
        for copy in copies[-2:]:
            copy.wait()
        if inner == 2:
            for k in range(1, outer):
                relay(k).wait_send()


def gather(nrow, ncol, pair, wt, qd, kv, block=8):
    R, C, width = pair.shape
    heads = wt.shape[0]
    return pl.pallas_call(
        functools.partial(gather_kernel, nrow, ncol),
        grid=(R // block,),
        out_shape=(
            jax.ShapeDtypeStruct((heads, R, C), jnp.float32),
            jax.ShapeDtypeStruct((ncol,) + qd.shape, qd.dtype),
            jax.ShapeDtypeStruct((nrow,) + kv.shape, kv.dtype),
        ),
        in_specs=[
            pl.BlockSpec((heads, width), lambda i: (0, 0)),
            pl.BlockSpec((block, C, width), lambda i: (i, 0, 0)),
            pl.BlockSpec(memory_space=pl.ANY),
            pl.BlockSpec(memory_space=pl.ANY),
        ],
        out_specs=(
            pl.BlockSpec((heads, block, C), lambda i: (0, i, 0)),
            pl.BlockSpec(memory_space=pl.ANY),
            pl.BlockSpec(memory_space=pl.ANY),
        ),
        scratch_shapes=[DMA((ncol,))] * 4 + [DMA((nrow,))] * 2 + [DMA((2,))],
        compiler_params=pltpu.CompilerParams(collective_id=0, has_side_effects=True),
    )(wt, pair, qd, kv)


def stats_kernel(ncol, st, out, got, back, s1, r1, s2, r2):
    row, col = lax.axis_index("row"), lax.axis_index("col")
    barrier = pltpu.get_barrier_semaphore()
    for k in range(1, ncol):
        pl.semaphore_signal(
            barrier, inc=1, device_id=(row, lax.rem(col + k, ncol)), device_id_type=MESH
        )
    pl.semaphore_wait(barrier, ncol - 1)
    sends = []
    for k in range(1, ncol):
        to = lax.rem(col + k, ncol)
        copy = remote(st.at[to], got.at[k], s1.at[k], r1.at[k], row, to)
        copy.start()
        sends.append(copy)
    got[0] = st[col]
    for k in range(1, ncol):
        remote(st.at[k], got.at[k], s1.at[k], r1.at[k], row, col).wait_recv()
    top = got[0, 0]
    for k in range(1, ncol):
        top = jnp.maximum(top, got[k, 0])
    total = jnp.zeros_like(top)
    upper = jnp.zeros_like(top)
    scales = []
    for k in range(ncol):
        scale = jnp.exp(got[k, 0] - top)
        scales.append(scale)
        total += got[k, 1] * scale
        upper += got[k, 2] * scale
    delta = upper / total
    for k in range(ncol):
        back[k, 0] = scales[k] / total
        back[k, 1] = delta
    for k in range(1, ncol):
        to = lax.rem(col + ncol - k, ncol)
        copy = remote(back.at[k], out.at[col], s2.at[k], r2.at[k], row, to)
        copy.start()
        sends.append(copy)
    out[col] = back[0]
    for k in range(1, ncol):
        src = lax.rem(col + k, ncol)
        remote(back.at[k], out.at[src], s2.at[k], r2.at[k], row, col).wait_recv()
    for copy in sends:
        copy.wait_send()


def stats(ncol, st):
    part = st.shape[2:]
    return pl.pallas_call(
        functools.partial(stats_kernel, ncol),
        out_shape=jax.ShapeDtypeStruct((ncol, 2) + part, jnp.float32),
        in_specs=[pl.BlockSpec(memory_space=VMEM)],
        out_specs=pl.BlockSpec(memory_space=VMEM),
        scratch_shapes=[
            VMEM((ncol, 3) + part, jnp.float32),
            VMEM((ncol, 2) + part, jnp.float32),
        ]
        + [DMA((ncol,))] * 4,
        compiler_params=pltpu.CompilerParams(collective_id=1, has_side_effects=True),
    )(st)


def reduce_kernel(
    nrow, ncol, wb, dq, dkv, wb_out, q_out, k_out, v_out,
    w1, w1sum, w2, w2sum, near, merged, far, kgot,
    ws1, wr1, ws2, wr2, ws3, wr3, ws4, wr4, ns, nr, qs, qr, ks, kr,
):
    row, col = lax.axis_index("row"), lax.axis_index("col")
    greet(nrow, ncol, row, col)
    sends = []

    def go(copy):
        copy.start()
        sends.append(copy)

    for k in range(1, nrow):
        to = lax.rem(row + k, nrow)
        go(remote(wb.at[to], w1.at[k], ws1.at[k], wr1.at[k], to, col))
    inner = 2 if ncol % 2 == 0 else 1
    outer = ncol // inner
    a, b = col // inner, lax.rem(col, inner)
    flip = a * inner + inner - 1 - b
    order = list(range(1, outer)) + [0]
    if inner == 2:
        for k in order:
            to = lax.rem(a + k, outer) * inner + 1 - b
            go(remote(dq.at[to], near.at[k], ns.at[k], nr.at[k], row, flip))
    for k in range(1, nrow):
        to = lax.rem(row + k, nrow)
        go(remote(dkv.at[to], kgot.at[k], ks.at[k], kr.at[k], to, col))
    total = wb[row]
    for k in range(1, nrow):
        remote(wb.at[0], w1.at[k], ws1.at[k], wr1.at[k], row, col).wait_recv()
        total += w1[k]
    w1sum[...] = total

    def pair_sum(k):
        value = dq[lax.rem(a + k, outer) * inner + b].astype(jnp.float32)
        if inner == 2:
            remote(dq.at[0], near.at[k], ns.at[k], nr.at[k], row, col).wait_recv()
            value += near[k].astype(jnp.float32)
        return value

    for k in range(1, ncol):
        to = lax.rem(col + k, ncol)
        go(remote(w1sum.at[to], w2.at[k], ws2.at[k], wr2.at[k], row, to))
    for k in range(1, outer):
        merged[k] = pair_sum(k).astype(merged.dtype)
        to = lax.rem(a + k, outer) * inner + b
        go(remote(merged.at[k], far.at[k], qs.at[k], qr.at[k], row, to))
    part = w1sum[col]
    for k in range(1, ncol):
        remote(w1sum.at[0], w2.at[k], ws2.at[k], wr2.at[k], row, col).wait_recv()
        part += w2[k]
    w2sum[...] = part
    for k in range(1, ncol):
        to = lax.rem(col + k, ncol)
        go(remote(w2sum, wb_out.at[row, col], ws3.at[k], wr3.at[k], row, to))
    wb_out[row, col] = part
    for k in range(1, ncol):
        src = lax.rem(col + ncol - k, ncol)
        remote(w2sum, wb_out.at[row, src], ws3.at[k], wr3.at[k], row, col).wait_recv()
    for k in range(1, nrow):
        to = lax.rem(row + k, nrow)
        go(remote(wb_out.at[row], wb_out.at[row], ws4.at[k], wr4.at[k], to, col))
    grad = dkv[row].astype(jnp.float32)
    for k in range(1, nrow):
        remote(dkv.at[0], kgot.at[k], ks.at[k], kr.at[k], row, col).wait_recv()
        grad += kgot[k].astype(jnp.float32)
    half = k_out.shape[1]
    k_out[...] = grad[:, :half].astype(k_out.dtype)
    v_out[...] = grad[:, half:].astype(v_out.dtype)
    grad = pair_sum(0)
    for k in range(1, outer):
        remote(merged.at[k], far.at[k], qs.at[k], qr.at[k], row, col).wait_recv()
        grad += far[k].astype(jnp.float32)
    q_out[...] = grad.astype(q_out.dtype)
    for k in range(1, nrow):
        src = lax.rem(row + nrow - k, nrow)
        remote(wb_out.at[src], wb_out.at[src], ws4.at[k], wr4.at[k], row, col).wait_recv()
    for copy in sends:
        copy.wait_send()


def reduce_all(nrow, ncol, wb, dq, dkv):
    chunk = wb.shape[2:]
    return pl.pallas_call(
        functools.partial(reduce_kernel, nrow, ncol),
        out_shape=(
            jax.ShapeDtypeStruct(wb.shape, jnp.float32),
            jax.ShapeDtypeStruct(dq.shape[1:], jnp.bfloat16),
            jax.ShapeDtypeStruct((dkv.shape[1], dkv.shape[2] // 2), jnp.bfloat16),
            jax.ShapeDtypeStruct((dkv.shape[1], dkv.shape[2] // 2), jnp.bfloat16),
        ),
        in_specs=[pl.BlockSpec(memory_space=VMEM)] * 3,
        out_specs=[pl.BlockSpec(memory_space=VMEM)] * 4,
        scratch_shapes=[
            VMEM(wb.shape, jnp.float32),
            VMEM((ncol,) + chunk, jnp.float32),
            VMEM((ncol,) + chunk, jnp.float32),
            VMEM(chunk, jnp.float32),
            VMEM(dq.shape, dq.dtype),
            VMEM(dq.shape, dq.dtype),
            VMEM(dq.shape, dq.dtype),
            VMEM(dkv.shape, dkv.dtype),
            DMA((nrow,)), DMA((nrow,)), DMA((ncol,)), DMA((ncol,)),
            DMA((ncol,)), DMA((ncol,)), DMA((nrow,)), DMA((nrow,)),
            DMA((ncol,)), DMA((ncol,)), DMA((ncol,)), DMA((ncol,)), DMA((nrow,)), DMA((nrow,)),
        ],
        compiler_params=pltpu.CompilerParams(collective_id=2, has_side_effects=True),
    )(wb, dq, dkv)


def pair_grad_kernel(wt, pair, ds, d_pair, wb):
    rows = pair.shape[0]
    by_row = jnp.swapaxes(ds[...].astype(jnp.float32), 0, 1).astype(jnp.bfloat16)

    @pl.when(pl.program_id(0) == 0)
    def _():
        wb[...] = jnp.zeros_like(wb)

    total = wb[...]
    for k in range(rows):
        one = by_row[k]
        d_pair[k] = lax.dot_general(
            one, wt[...], (((0,), (0,)), ((), ())), preferred_element_type=jnp.float32
        ).astype(jnp.bfloat16)
        total += jnp.dot(one, pair[k], preferred_element_type=jnp.float32)
    wb[...] = total


def pair_grad(pair, wt, ds, block=16):
    R, C, width = pair.shape
    heads = wt.shape[0]
    return pl.pallas_call(
        pair_grad_kernel,
        grid=(R // block,),
        out_shape=(
            jax.ShapeDtypeStruct(pair.shape, jnp.bfloat16),
            jax.ShapeDtypeStruct((heads, width), jnp.float32),
        ),
        in_specs=[
            pl.BlockSpec((heads, width), lambda i: (0, 0)),
            pl.BlockSpec((block, C, width), lambda i: (i, 0, 0)),
            pl.BlockSpec((heads, block, C), lambda i: (0, i, 0)),
        ],
        out_specs=(
            pl.BlockSpec((block, C, width), lambda i: (i, 0, 0)),
            pl.BlockSpec((heads, width), lambda i: (0, 0)),
        ),
    )(wt, pair, ds)


def on_device(nrow, ncol, pair, w_bias, queries, keys, values, d_out):
    R, C, width = pair.shape
    dcol, drow = queries.shape[1], keys.shape[1]
    wt = w_bias.T
    pair_bias, qd_all, kv_all = gather(
        nrow, ncol, pair, wt,
        jnp.concatenate([queries, d_out], axis=1),
        jnp.concatenate([keys, values], axis=1),
    )
    query_heads = qd_all[:, :, :dcol].transpose(1, 0, 2).reshape(R, H, HD)
    out_heads = qd_all[:, :, dcol:].transpose(1, 0, 2).reshape(R, H, HD)
    key_heads = kv_all[:, :, :drow].transpose(1, 0, 2).reshape(C, H, HD)
    value_heads = kv_all[:, :, drow:].transpose(1, 0, 2).reshape(C, H, HD)
    scores = jnp.einsum(
        "ihd,jhd->hij", query_heads, key_heads, preferred_element_type=jnp.float32
    ) * SCALE + pair_bias
    grad_prob = jnp.einsum(
        "ihd,jhd->hij", out_heads, value_heads, preferred_element_type=jnp.float32
    )
    local_max = jnp.max(scores, axis=-1)
    exp_scores = jnp.exp(scores - local_max[..., None])
    st = jnp.stack(
        [local_max, jnp.sum(exp_scores, axis=-1), jnp.sum(exp_scores * grad_prob, axis=-1)]
    )
    count = H // ncol * R
    lanes = 128 if count % 128 == 0 else R
    st = st.reshape(3, ncol, count // lanes, lanes).transpose(1, 0, 2, 3)
    back = stats(ncol, st).transpose(1, 0, 2, 3).reshape(2, H, R)
    weights = exp_scores * back[0][..., None]
    grad_score = (weights * (grad_prob - back[1][..., None])).astype(jnp.bfloat16)
    weights_low = weights.astype(jnp.bfloat16)
    d_pair, weight_term = pair_grad(pair, wt, grad_score)
    query_term = jnp.einsum(
        "hij,jhd->ihd", grad_score, key_heads, preferred_element_type=jnp.float32
    ) * SCALE
    key_term = jnp.einsum(
        "hij,ihd->jhd", grad_score, query_heads, preferred_element_type=jnp.float32
    ) * SCALE
    value_term = jnp.einsum(
        "hij,ihd->jhd", weights_low, out_heads, preferred_element_type=jnp.float32
    )
    dq = query_term.astype(jnp.bfloat16).reshape(R, ncol, dcol).transpose(1, 0, 2)
    if R * dcol % 2048 == 0:
        dq = dq.reshape(ncol, R * dcol // 128, 128)
    dk = key_term.astype(jnp.bfloat16).reshape(C, nrow, drow).transpose(1, 0, 2)
    dv = value_term.astype(jnp.bfloat16).reshape(C, nrow, drow).transpose(1, 0, 2)
    wb = weight_term.reshape(ncol, H // ncol, nrow, width // nrow).transpose(2, 0, 1, 3)
    wb, q_grad, k_grad, v_grad = reduce_all(nrow, ncol, wb, dq, jnp.concatenate([dk, dv], axis=2))
    d_wbias = wb.transpose(0, 3, 1, 2).reshape(width, H)
    return d_pair, d_wbias, q_grad.reshape(R, dcol), k_grad, v_grad


def solution(mesh):
    return jax.shard_map(
        functools.partial(on_device, mesh.shape["row"], mesh.shape["col"]),
        mesh=mesh,
        in_specs=(
            P("row", "col", None),
            P(),
            P("row", "col"),
            P("col", "row"),
            P("col", "row"),
            P("row", "col"),
        ),
        out_specs=(P("row", "col", None), P(), P("row", "col"), P("col", "row"), P("col", "row")),
        check_vma=False,
    )
```

```python
import functools

import jax
import jax.numpy as jnp
from jax import lax
from jax.experimental import pallas as pl
from jax.experimental.pallas import tpu as pltpu
from jax.sharding import PartitionSpec as P

H = 96
HD = 16
SCALE = 1.0 / HD**0.5
MESH = pl.DeviceIdType.MESH
VMEM = pltpu.VMEM
DMA = pltpu.SemaphoreType.DMA


def remote(src, dst, send, recv, row, col):
    return pltpu.make_async_remote_copy(
        src_ref=src, dst_ref=dst, send_sem=send, recv_sem=recv,
        device_id=(row, col), device_id_type=MESH,
    )


def greet(nrow, ncol, row, col):
    barrier = pltpu.get_barrier_semaphore()
    for k in range(1, ncol):
        pl.semaphore_signal(
            barrier, inc=1, device_id=(row, lax.rem(col + k, ncol)), device_id_type=MESH
        )
    for k in range(1, nrow):
        pl.semaphore_signal(
            barrier, inc=1, device_id=(lax.rem(row + k, nrow), col), device_id_type=MESH
        )
    pl.semaphore_wait(barrier, ncol + nrow - 2)


def gather_kernel(
    nrow, ncol, wt, pair, q, k_in, v, d, out, qd_all, kv_all,
    qd, kv, qs, qr, fs, fr, ks, kr, own,
):
    row, col = lax.axis_index("row"), lax.axis_index("col")
    inner = 2 if ncol % 2 == 0 else 1
    outer = ncol // inner
    a, b = col // inner, lax.rem(col, inner)
    flip = a * inner + inner - 1 - b
    step, last = pl.program_id(0), pl.num_programs(0) - 1
    steps = out.shape[1]

    def sends():
        copies = []
        for k in range(1, outer):
            to = lax.rem(a + k, outer) * inner + b
            copies.append(remote(qd, qd_all.at[col], qs.at[k], qr.at[k], row, to))
        if inner == 2:
            copies.append(remote(qd, qd_all.at[col], fs.at[0], fr.at[0], row, flip))
        for k in range(1, nrow):
            to = lax.rem(row + k, nrow)
            copies.append(remote(kv, kv_all.at[row], ks.at[k], kr.at[k], to, col))
        copies.append(pltpu.make_async_copy(qd, qd_all.at[col], own.at[0]))
        copies.append(pltpu.make_async_copy(kv, kv_all.at[row], own.at[1]))
        return copies

    def relay(k):
        src = lax.rem(a + outer - k, outer) * inner + b
        return remote(qd_all.at[src], qd_all.at[src], fs.at[k], fr.at[k], row, flip)

    @pl.when(step == 0)
    def _():
        qd[...] = jnp.concatenate([q[...], d[...]], axis=1)
        kv[...] = jnp.concatenate([k_in[...], v[...]], axis=1)
        greet(nrow, ncol, row, col)
        for copy in sends():
            copy.start()

    out[...] = jnp.swapaxes(
        jnp.stack(
            [
                lax.dot_general(
                    wt[...], pair[k], (((1,), (1,)), ((), ())),
                    preferred_element_type=jnp.float32,
                )
                for k in range(steps)
            ]
        ),
        0, 1,
    )

    for k in range(1, outer):

        @pl.when(step == jnp.minimum(last, (last + 1) // 2 + 2 * (k - 1)))
        def _():
            src = lax.rem(a + outer - k, outer) * inner + b
            remote(qd, qd_all.at[src], qs.at[k], qr.at[k], row, col).wait_recv()
            if inner == 2:
                relay(k).start()

    @pl.when(step == last)
    def _():
        if inner == 2:
            for k in range(outer):
                src = lax.rem(a + outer - k, outer) * inner + 1 - b
                remote(qd, qd_all.at[src], fs.at[k], fr.at[k], row, col).wait_recv()
        for k in range(1, nrow):
            src = lax.rem(row + nrow - k, nrow)
            remote(kv, kv_all.at[src], ks.at[k], kr.at[k], row, col).wait_recv()
        copies = sends()
        for copy in copies[:-2]:
            copy.wait_send()
        for copy in copies[-2:]:
            copy.wait()
        if inner == 2:
            for k in range(1, outer):
                relay(k).wait_send()


def gather(nrow, ncol, pair, wt, q, k, v, d, block=8):
    R, C, width = pair.shape
    qd = jax.ShapeDtypeStruct((R, 2 * q.shape[1]), q.dtype)
    kv = jax.ShapeDtypeStruct((C, 2 * k.shape[1]), k.dtype)
    heads = wt.shape[0]
    return pl.pallas_call(
        functools.partial(gather_kernel, nrow, ncol),
        grid=(R // block,),
        out_shape=(
            jax.ShapeDtypeStruct((heads, R, C), jnp.float32),
            jax.ShapeDtypeStruct((ncol,) + qd.shape, qd.dtype),
            jax.ShapeDtypeStruct((nrow,) + kv.shape, kv.dtype),
        ),
        in_specs=[
            pl.BlockSpec((heads, width), lambda i: (0, 0)),
            pl.BlockSpec((block, C, width), lambda i: (i, 0, 0)),
        ]
        + [pl.BlockSpec(memory_space=VMEM)] * 4,
        out_specs=(
            pl.BlockSpec((heads, block, C), lambda i: (0, i, 0)),
            pl.BlockSpec(memory_space=pl.ANY),
            pl.BlockSpec(memory_space=pl.ANY),
        ),
        scratch_shapes=[VMEM(qd.shape, qd.dtype), VMEM(kv.shape, kv.dtype)]
        + [DMA((ncol,))] * 4 + [DMA((nrow,))] * 2 + [DMA((2,))],
        compiler_params=pltpu.CompilerParams(collective_id=0, has_side_effects=True),
    )(wt, pair, q, k, v, d)


def stats_kernel(ncol, st, out, got, back, s1, r1, s2, r2):
    row, col = lax.axis_index("row"), lax.axis_index("col")
    barrier = pltpu.get_barrier_semaphore()
    for k in range(1, ncol):
        pl.semaphore_signal(
            barrier, inc=1, device_id=(row, lax.rem(col + k, ncol)), device_id_type=MESH
        )
    pl.semaphore_wait(barrier, ncol - 1)
    sends = []
    for k in range(1, ncol):
        to = lax.rem(col + k, ncol)
        copy = remote(st.at[to], got.at[k], s1.at[k], r1.at[k], row, to)
        copy.start()
        sends.append(copy)
    got[0] = st[col]
    for k in range(1, ncol):
        remote(st.at[k], got.at[k], s1.at[k], r1.at[k], row, col).wait_recv()
    top = got[0, 0]
    for k in range(1, ncol):
        top = jnp.maximum(top, got[k, 0])
    total = jnp.zeros_like(top)
    upper = jnp.zeros_like(top)
    scales = []
    for k in range(ncol):
        scale = jnp.exp(got[k, 0] - top)
        scales.append(scale)
        total += got[k, 1] * scale
        upper += got[k, 2] * scale
    delta = upper / total
    for k in range(ncol):
        back[k, 0] = scales[k] / total
        back[k, 1] = delta
    for k in range(1, ncol):
        to = lax.rem(col + ncol - k, ncol)
        copy = remote(back.at[k], out.at[col], s2.at[k], r2.at[k], row, to)
        copy.start()
        sends.append(copy)
    out[col] = back[0]
    for k in range(1, ncol):
        src = lax.rem(col + k, ncol)
        remote(back.at[k], out.at[src], s2.at[k], r2.at[k], row, col).wait_recv()
    for copy in sends:
        copy.wait_send()


def stats(ncol, st):
    part = st.shape[2:]
    return pl.pallas_call(
        functools.partial(stats_kernel, ncol),
        out_shape=jax.ShapeDtypeStruct((ncol, 2) + part, jnp.float32),
        in_specs=[pl.BlockSpec(memory_space=VMEM)],
        out_specs=pl.BlockSpec(memory_space=VMEM),
        scratch_shapes=[
            VMEM((ncol, 3) + part, jnp.float32),
            VMEM((ncol, 2) + part, jnp.float32),
        ]
        + [DMA((ncol,))] * 4,
        compiler_params=pltpu.CompilerParams(collective_id=1, has_side_effects=True),
    )(st)


def reduce_kernel(
    nrow, ncol, wb, dq, dkv, wb_out, q_out, k_out, v_out,
    w1, w1sum, w2, w2sum, near, merged, far, kgot,
    ws1, wr1, ws2, wr2, ws3, wr3, ws4, wr4, ns, nr, qs, qr, ks, kr,
):
    row, col = lax.axis_index("row"), lax.axis_index("col")
    greet(nrow, ncol, row, col)
    sends = []

    def go(copy):
        copy.start()
        sends.append(copy)

    for k in range(1, nrow):
        to = lax.rem(row + k, nrow)
        go(remote(wb.at[to], w1.at[k], ws1.at[k], wr1.at[k], to, col))
    inner = 2 if ncol % 2 == 0 else 1
    outer = ncol // inner
    a, b = col // inner, lax.rem(col, inner)
    flip = a * inner + inner - 1 - b
    order = list(range(1, outer)) + [0]
    if inner == 2:
        for k in order:
            to = lax.rem(a + k, outer) * inner + 1 - b
            go(remote(dq.at[to], near.at[k], ns.at[k], nr.at[k], row, flip))
    for k in range(1, nrow):
        to = lax.rem(row + k, nrow)
        go(remote(dkv.at[to], kgot.at[k], ks.at[k], kr.at[k], to, col))
    total = wb[row]
    for k in range(1, nrow):
        remote(wb.at[0], w1.at[k], ws1.at[k], wr1.at[k], row, col).wait_recv()
        total += w1[k]
    w1sum[...] = total

    def pair_sum(k):
        value = dq[lax.rem(a + k, outer) * inner + b].astype(jnp.float32)
        if inner == 2:
            remote(dq.at[0], near.at[k], ns.at[k], nr.at[k], row, col).wait_recv()
            value += near[k].astype(jnp.float32)
        return value

    for k in range(1, ncol):
        to = lax.rem(col + k, ncol)
        go(remote(w1sum.at[to], w2.at[k], ws2.at[k], wr2.at[k], row, to))
    for k in range(1, outer):
        merged[k] = pair_sum(k).astype(merged.dtype)
        to = lax.rem(a + k, outer) * inner + b
        go(remote(merged.at[k], far.at[k], qs.at[k], qr.at[k], row, to))
    part = w1sum[col]
    for k in range(1, ncol):
        remote(w1sum.at[0], w2.at[k], ws2.at[k], wr2.at[k], row, col).wait_recv()
        part += w2[k]
    w2sum[...] = part
    for k in range(1, ncol):
        to = lax.rem(col + k, ncol)
        go(remote(w2sum, wb_out.at[row, col], ws3.at[k], wr3.at[k], row, to))
    wb_out[row, col] = part
    for k in range(1, ncol):
        src = lax.rem(col + ncol - k, ncol)
        remote(w2sum, wb_out.at[row, src], ws3.at[k], wr3.at[k], row, col).wait_recv()
    for k in range(1, nrow):
        to = lax.rem(row + k, nrow)
        go(remote(wb_out.at[row], wb_out.at[row], ws4.at[k], wr4.at[k], to, col))
    grad = dkv[row].astype(jnp.float32)
    for k in range(1, nrow):
        remote(dkv.at[0], kgot.at[k], ks.at[k], kr.at[k], row, col).wait_recv()
        grad += kgot[k].astype(jnp.float32)
    half = k_out.shape[1]
    k_out[...] = grad[:, :half].astype(k_out.dtype)
    v_out[...] = grad[:, half:].astype(v_out.dtype)
    grad = pair_sum(0)
    for k in range(1, outer):
        remote(merged.at[k], far.at[k], qs.at[k], qr.at[k], row, col).wait_recv()
        grad += far[k].astype(jnp.float32)
    q_out[...] = grad.astype(q_out.dtype)
    for k in range(1, nrow):
        src = lax.rem(row + nrow - k, nrow)
        remote(wb_out.at[src], wb_out.at[src], ws4.at[k], wr4.at[k], row, col).wait_recv()
    for copy in sends:
        copy.wait_send()


def reduce_all(nrow, ncol, wb, dq, dkv):
    chunk = wb.shape[2:]
    return pl.pallas_call(
        functools.partial(reduce_kernel, nrow, ncol),
        out_shape=(
            jax.ShapeDtypeStruct(wb.shape, jnp.float32),
            jax.ShapeDtypeStruct(dq.shape[1:], jnp.bfloat16),
            jax.ShapeDtypeStruct((dkv.shape[1], dkv.shape[2] // 2), jnp.bfloat16),
            jax.ShapeDtypeStruct((dkv.shape[1], dkv.shape[2] // 2), jnp.bfloat16),
        ),
        in_specs=[pl.BlockSpec(memory_space=VMEM)] * 3,
        out_specs=[pl.BlockSpec(memory_space=VMEM)] * 4,
        scratch_shapes=[
            VMEM(wb.shape, jnp.float32),
            VMEM((ncol,) + chunk, jnp.float32),
            VMEM((ncol,) + chunk, jnp.float32),
            VMEM(chunk, jnp.float32),
            VMEM(dq.shape, dq.dtype),
            VMEM(dq.shape, dq.dtype),
            VMEM(dq.shape, dq.dtype),
            VMEM(dkv.shape, dkv.dtype),
            DMA((nrow,)), DMA((nrow,)), DMA((ncol,)), DMA((ncol,)),
            DMA((ncol,)), DMA((ncol,)), DMA((nrow,)), DMA((nrow,)),
            DMA((ncol,)), DMA((ncol,)), DMA((ncol,)), DMA((ncol,)), DMA((nrow,)), DMA((nrow,)),
        ],
        compiler_params=pltpu.CompilerParams(collective_id=2, has_side_effects=True),
    )(wb, dq, dkv)


def pair_grad_kernel(wt, pair, ds, d_pair, wb):
    rows = pair.shape[0]
    cols, width = pair.shape[1:]
    by_row = jnp.swapaxes(ds[...].astype(jnp.float32), 0, 1)
    flat = jnp.swapaxes(by_row, 1, 2).astype(jnp.bfloat16).reshape(rows * cols, -1)

    @pl.when(pl.program_id(0) == 0)
    def _():
        wb[...] = jnp.zeros_like(wb)

    d_pair[...] = (
        jnp.dot(flat, wt[...], preferred_element_type=jnp.float32)
        .astype(jnp.bfloat16)
        .reshape(rows, cols, width)
    )
    wb[...] += lax.dot_general(
        flat, pair[...].reshape(rows * cols, width), (((0,), (0,)), ((), ())),
        preferred_element_type=jnp.float32,
    )


def pair_grad(pair, wt, ds, block=16):
    R, C, width = pair.shape
    heads = wt.shape[0]
    return pl.pallas_call(
        pair_grad_kernel,
        grid=(R // block,),
        out_shape=(
            jax.ShapeDtypeStruct(pair.shape, jnp.bfloat16),
            jax.ShapeDtypeStruct((heads, width), jnp.float32),
        ),
        in_specs=[
            pl.BlockSpec((heads, width), lambda i: (0, 0)),
            pl.BlockSpec((block, C, width), lambda i: (i, 0, 0)),
            pl.BlockSpec((heads, block, C), lambda i: (0, i, 0)),
        ],
        out_specs=(
            pl.BlockSpec((block, C, width), lambda i: (i, 0, 0)),
            pl.BlockSpec((heads, width), lambda i: (0, 0)),
        ),
    )(wt, pair, ds)


def on_device(nrow, ncol, pair, w_bias, queries, keys, values, d_out):
    R, C, width = pair.shape
    dcol, drow = queries.shape[1], keys.shape[1]
    wt = w_bias.T
    pair_bias, qd_all, kv_all = gather(
        nrow, ncol, pair, wt,
        queries, keys, values, d_out,
    )
    query_heads = qd_all[:, :, :dcol].transpose(1, 0, 2).reshape(R, H, HD)
    out_heads = qd_all[:, :, dcol:].transpose(1, 0, 2).reshape(R, H, HD)
    key_heads = kv_all[:, :, :drow].transpose(1, 0, 2).reshape(C, H, HD)
    value_heads = kv_all[:, :, drow:].transpose(1, 0, 2).reshape(C, H, HD)
    scores = jnp.einsum(
        "ihd,jhd->hij", query_heads, key_heads, preferred_element_type=jnp.float32
    ) * SCALE + pair_bias
    grad_prob = jnp.einsum(
        "ihd,jhd->hij", out_heads, value_heads, preferred_element_type=jnp.float32
    )
    local_max = jnp.max(scores, axis=-1)
    exp_scores = jnp.exp(scores - local_max[..., None])
    st = jnp.stack(
        [local_max, jnp.sum(exp_scores, axis=-1), jnp.sum(exp_scores * grad_prob, axis=-1)]
    )
    count = H // ncol * R
    lanes = 128 if count % 128 == 0 else R
    st = st.reshape(3, ncol, count // lanes, lanes).transpose(1, 0, 2, 3)
    back = stats(ncol, st).transpose(1, 0, 2, 3).reshape(2, H, R)
    weights = exp_scores * back[0][..., None]
    grad_score = (weights * (grad_prob - back[1][..., None])).astype(jnp.bfloat16)
    weights_low = weights.astype(jnp.bfloat16)
    d_pair, weight_term = pair_grad(pair, wt, grad_score)
    query_term = jnp.einsum(
        "hij,jhd->ihd", grad_score, key_heads, preferred_element_type=jnp.float32
    ) * SCALE
    key_term = jnp.einsum(
        "hij,ihd->jhd", grad_score, query_heads, preferred_element_type=jnp.float32
    ) * SCALE
    value_term = jnp.einsum(
        "hij,ihd->jhd", weights_low, out_heads, preferred_element_type=jnp.float32
    )
    dq = query_term.astype(jnp.bfloat16).reshape(R, ncol, dcol).transpose(1, 0, 2)
    if R * dcol % 2048 == 0:
        dq = dq.reshape(ncol, R * dcol // 128, 128)
    dk = key_term.astype(jnp.bfloat16).reshape(C, nrow, drow).transpose(1, 0, 2)
    dv = value_term.astype(jnp.bfloat16).reshape(C, nrow, drow).transpose(1, 0, 2)
    wb = weight_term.reshape(ncol, H // ncol, nrow, width // nrow).transpose(2, 0, 1, 3)
    wb, q_grad, k_grad, v_grad = reduce_all(nrow, ncol, wb, dq, jnp.concatenate([dk, dv], axis=2))
    d_wbias = wb.transpose(0, 3, 1, 2).reshape(width, H)
    return d_pair, d_wbias, q_grad.reshape(R, dcol), k_grad, v_grad


def solution(mesh):
    return jax.shard_map(
        functools.partial(on_device, mesh.shape["row"], mesh.shape["col"]),
        mesh=mesh,
        in_specs=(
            P("row", "col", None),
            P(),
            P("row", "col"),
            P("col", "row"),
            P("col", "row"),
            P("row", "col"),
        ),
        out_specs=(P("row", "col", None), P(), P("row", "col"), P("col", "row"), P("col", "row")),
        check_vma=False,
    )
```
